32 devices in a mesh: dp: 4 (over z), lib: 8 (over y, x, core).
Axes of the slice: x: 2, y: 2, z: 4, core: 2. Of those that a mesh axis runs over, the one named last changes fastest.
Arguments:
- spectra: bfloat16 [12288, 512], P(('dp', 'lib')), may hold values from -6 to 6
- w_proj: bfloat16 [512, 512], replicated, may hold values from -0.25 to 0.25
- fixed_library_matrix: bfloat16 [8192, 512], P('lib')
- mol_rows: bfloat16 [65536, 512], P(('dp', 'lib'))
- cand_ids: int32 [12288, 4], P(('dp', 'lib')), may hold values from 0 to 65535, as said below
- iso_count: int32 [12288], P(('dp', 'lib')), may hold values from 1 to 3
Outputs:
- grad_w: float32 [512, 512], replicated
- grad_mol: float32 [65536, 512], P(('dp', 'lib'))
- loss: float32 [], replicated
The draws below stay inside these ranges and needn't reach their ends.
Inputs may be any that keep to these rules, and one draw needn't show every extreme that they name: cand_ids of a spectrum on device dp, lib (in dp+lib order) name rows of the dp group's molecules: id // 2048 // 8 equals dp. Over one device's 1536 slots (all columns, live or not), at most 384 name rows whose (id // 2048) % 8 is one lib index, and exactly 384 for some lib index on every device.
All inputs are finite; a program needn't handle non-finite values.
Results may differ from the reference program's by a relative error of at most 0.0074.
Values may be sent and summed in bfloat16 or wider, within the bound.
No kernel may reach another device: no remote copies, remote signals or barrier semaphores. Data moves between devices by JAX's collectives and lax.ppermute only.
A program may use at most 64 MiB of HBM per device.

```python
import jax
import jax.numpy as jnp
from jax import lax

D = 512
Q_DEV = 384
MOL_DEV = 2048
ISO = 3
QUERIES = 12288
BANK = 8192
MOLS = 65536
SLOTS = 1536
CAP = 384
N_LIB = 8


def draw_fixed_library_matrix(key, part):
    key_base, key_scale = jax.random.split(key, 2)
    normal_part = jax.random.normal(key_base, (BANK, D), jnp.float32)
    row_scale = jnp.exp(jax.random.uniform(key_scale, (BANK, 1), jnp.float32, jnp.log(0.2), jnp.log(0.3)))
    return (normal_part * row_scale).astype(jnp.bfloat16)


def draw_mol_rows(key, part):
    own_key = jax.random.fold_in(key, 101)
    key_base, key_scale = jax.random.split(own_key, 2)
    base = jax.random.normal(key_base, (MOLS, D), jnp.float32)
    row_scale = jnp.exp(jax.random.uniform(key_scale, (MOLS, 1), jnp.float32, jnp.log(0.1), jnp.log(3.0)))
    return (base * row_scale).astype(jnp.bfloat16)


def draw_cand_ids(key, part):
    blocks = QUERIES // Q_DEV
    key_owner, key_slot, key_local = jax.random.split(key, 3)
    rest = SLOTS - CAP
    base = rest // (N_LIB - 1)
    spare = rest % (N_LIB - 1)
    rank = jnp.arange(N_LIB, dtype=jnp.int32)
    counts = jnp.where(rank == 0, CAP, base + (rank - 1 < spare).astype(jnp.int32))
    bounds = jnp.cumsum(counts)
    slots = jnp.arange(SLOTS, dtype=jnp.int32)
    rank_of_slot = jnp.sum((bounds[None, :] <= slots[:, None]).astype(jnp.int32), axis=1)
    owner_scores = jax.random.randint(key_owner, (blocks, N_LIB), 0, 1 << 20) * N_LIB + rank[None, :]
    owner_order = jnp.argsort(owner_scores, axis=1).astype(jnp.int32)
    slot_scores = jax.random.randint(key_slot, (blocks, SLOTS), 0, 1 << 16) * SLOTS + slots[None, :]
    shuffle = jnp.argsort(slot_scores, axis=1).astype(jnp.int32)
    shuffled_rank = rank_of_slot[shuffle]
    owner = jnp.take_along_axis(owner_order, shuffled_rank, axis=1)
    local = jax.random.randint(key_local, (blocks, SLOTS), 0, MOL_DEV)
    block_ids = jnp.arange(blocks, dtype=jnp.int32)[:, None]
    group = block_ids // N_LIB
    ids = (group * N_LIB + owner) * MOL_DEV + local
    return ids.reshape(QUERIES, 1 + ISO).astype(jnp.int32)


def with_ends(entries, key, smallest, largest):
    longest = entries.shape.index(max(entries.shape))
    spots = []
    for shift in (0, 1):
        where = [jax.random.randint(jax.random.fold_in(key, axis), (), 0, length) for axis, length in enumerate(entries.shape)]
        where[longest] = (where[longest] + shift) % entries.shape[longest]
        spots.append(tuple(where))
    return entries.at[spots[0]].set(smallest).at[spots[1]].set(largest)


def steps_of(rng, extent, shards, low, high):
    level, own = 1.0, jax.random.fold_in(rng, 6)
    for dim, shards_of in shards:
        draws = jnp.exp(jax.random.uniform(jax.random.fold_in(own, dim), (shards_of,), jnp.float32, low / len(shards), high / len(shards)))
        level = level * jnp.repeat(draws, extent[dim] // shards_of).reshape([-1 if axis == dim else 1 for axis in range(len(extent))])
    return level


def normal_values(key, extent, deviation, reach, pieces=(), held_as=jnp.bfloat16):
    result = jax.random.normal(key, extent, jnp.float32) * deviation
    if len(pieces) > 0:
        result = steps_of(key, extent, pieces, -0.22, 0.18) * result
    return jnp.clip(result, min=-reach, max=reach).astype(held_as)


def setup_inputs(seed: int = 0) -> dict:
    arg_keys = jax.random.split(jax.random.key(seed), 7)
    spectra = normal_values(arg_keys[0], (QUERIES, D), 1.0, 6.0, ((0, 32),))
    w_proj = normal_values(arg_keys[1], (D, D), D ** -0.5, 0.25)
    fixed_library_matrix = draw_fixed_library_matrix(jax.random.fold_in(arg_keys[6], 71), 0)
    mol_rows = draw_mol_rows(jax.random.fold_in(arg_keys[6], 71), 0)
    cand_ids = draw_cand_ids(jax.random.fold_in(arg_keys[6], 71), 0)
    iso_count = with_ends(jax.random.randint(arg_keys[5], (QUERIES,), 1, ISO + 1), jax.random.fold_in(arg_keys[5], 1), 1, ISO).astype(jnp.int32)
    return dict(spectra=spectra, w_proj=w_proj, fixed_library_matrix=fixed_library_matrix, mol_rows=mol_rows, cand_ids=cand_ids, iso_count=iso_count)


sharpness_divisor = 0.07

def reference(spectra, w_proj, fixed_library_matrix, mol_rows, cand_ids, iso_count):
    u_proj = jnp.dot(spectra, w_proj, preferred_element_type=jnp.float32)
    norm_all = jnp.sqrt(lax.optimization_barrier(jnp.sum(u_proj * u_proj, axis=1, keepdims=True)) + 1e-06)
    unit_all = u_proj / norm_all
    query_all = unit_all.astype(jnp.bfloat16)
    column = jnp.arange(1 + ISO, dtype=jnp.int32)[None, :]
    live_all = column <= iso_count[:, None]
    first = (column == 0).astype(jnp.float32)

    def one_block(index):
        start = (index * Q_DEV).astype(jnp.int32)
        spectrum_encoding = lax.dynamic_slice_in_dim(query_all, start, Q_DEV, 0)
        normalized_spectrum_matrix = lax.dynamic_slice_in_dim(unit_all, start, Q_DEV, 0)
        norm = lax.dynamic_slice_in_dim(norm_all, start, Q_DEV, 0)
        live = lax.dynamic_slice_in_dim(live_all, start, Q_DEV, 0)
        ids = lax.dynamic_slice_in_dim(cand_ids, start, Q_DEV, 0)
        contender_embedding_matrix = mol_rows[ids].astype(jnp.float32)
        contender_similarity_values = jnp.einsum('ti,tmi->tm', spectrum_encoding.astype(jnp.float32), contender_embedding_matrix) / sharpness_divisor
        library_similarity_values = jnp.dot(spectrum_encoding, fixed_library_matrix.T, preferred_element_type=jnp.float32) / sharpness_divisor
        top = jnp.maximum(lax.optimization_barrier(jnp.max(jnp.where(live, contender_similarity_values, -1e+30), axis=1)), lax.optimization_barrier(jnp.max(library_similarity_values, axis=1)))
        weight_cand = jnp.where(live, jnp.exp(contender_similarity_values - top[:, None]), 0.0)
        weight_bank = jnp.exp(library_similarity_values - top[:, None])
        objective_aggregate = lax.optimization_barrier(jnp.sum(weight_cand, axis=1)) + lax.optimization_barrier(jnp.sum(weight_bank, axis=1))
        derivative_tally = jnp.dot(weight_bank.astype(jnp.bfloat16), fixed_library_matrix, preferred_element_type=jnp.float32)
        derivative_tally = derivative_tally + jnp.einsum('qk,qkd->qd', weight_cand, contender_embedding_matrix)
        lse = top + jnp.log(objective_aggregate)
        losses = lse - contender_similarity_values[:, 0]
        spectrum_derivative = (derivative_tally / objective_aggregate[:, None] - contender_embedding_matrix[:, 0, :]) / sharpness_divisor
        grad_u = (spectrum_derivative - normalized_spectrum_matrix * lax.optimization_barrier(jnp.sum(normalized_spectrum_matrix * spectrum_derivative, axis=1, keepdims=True))) / norm
        inverse_sharpness = jnp.where(live, weight_cand / objective_aggregate[:, None] - first, 0.0)
        contender_derivative = (inverse_sharpness[:, :, None] * normalized_spectrum_matrix[:, None, :] / sharpness_divisor).astype(jnp.bfloat16)
        return (losses, grad_u.astype(jnp.bfloat16), contender_derivative)
    blocks = jnp.arange(QUERIES // Q_DEV, dtype=jnp.int32)
    losses, grad_u, contender_derivative = lax.map(one_block, blocks)
    grad_u = grad_u.reshape(QUERIES, D)
    grad_w = jnp.dot(spectra.T, grad_u, preferred_element_type=jnp.float32)
    grad_mol = jnp.zeros((MOLS, D), jnp.float32).at[cand_ids.reshape(-1)].add(contender_derivative.reshape(-1, D).astype(jnp.float32))
    loss = jnp.sum(losses) / QUERIES
    return (grad_w, grad_mol, loss)
```

```python
import functools

import jax
import jax.numpy as jnp
from jax import lax
from jax.experimental import pallas as pl
from jax.experimental.pallas import tpu as pltpu
from jax.sharding import PartitionSpec as P


sharpness_divisor = 0.07
INV = 1.0 / sharpness_divisor
INV_LOG2 = 1.4426950408889634 / sharpness_divisor
BASE = 256
F32 = jnp.float32
BF16 = jnp.bfloat16
VMEM_BYTES = 24 * 1024 * 1024
ROOM_BYTES = 36 * 1024 * 1024
PIECES = 4


def nt(a, b):
    return lax.dot_general(a, b, (((1,), (1,)), ((), ())), preferred_element_type=F32)


def nn(a, b):
    return lax.dot_general(a, b, (((1,), (0,)), ((), ())), preferred_element_type=F32)


def tree(terms):
    while len(terms) > 1:
        terms = [a + b for a, b in zip(terms[::2], terms[1::2])]
    return terms[0]


def turn_kernel(bank_ref, mol_ref, bankt_ref, molt_ref):
    for src, dst in ((bank_ref, bankt_ref), (mol_ref, molt_ref)):
        for r in range(0, src.shape[0], 256):
            dst[:, r : r + 256] = src[r : r + 256, :].T


def score_kernel(rows, lanes, mol_tile, at_lane, aliased, *refs):
    own_ref, xa_ref, xb_ref, w_ref, bank_ref, mol_ref = refs[:6]
    refs = refs[6 + aliased :]
    qt_ref, sp_ref, wbt_ref, st_ref, lse_ref, bs_ref, wt_ref = refs
    mol_count = mol_ref.shape[0]
    pair = 2 * rows
    sp_ref[at_lane : at_lane + rows, :] = xa_ref[:rows, :]
    sp_ref[at_lane + rows : at_lane + pair, :] = xb_ref[:rows, :]
    wt_ref[...] = w_ref[...].T
    digits = jnp.concatenate(
        [xa_ref[rows : rows + 16, :rows].astype(F32), xb_ref[rows : rows + 16, :rows].astype(F32)],
        axis=1,
    )
    base = (own_ref[0] * mol_count).astype(F32)
    local = digits[0:4] * BASE + digits[4:8] - base
    local = jnp.where((local >= 0) & (local < mol_count), local, -1.0)
    for c in range(0, pair, lanes):
        cols = slice(c, c + lanes)
        out = slice(at_lane + c, at_lane + c + lanes)
        ut = nt(wt_ref[...], sp_ref[out, :])
        norm = jnp.sqrt(jnp.sum(ut * ut, axis=0, keepdims=True) + 1e-06)
        qt = (ut * (1.0 / norm)).astype(BF16)
        qt_ref[:, out] = qt
        here_at = local[:, cols]
        at = here_at.astype(jnp.int32)
        at = jnp.concatenate([at, at], axis=0)
        group = at >> 3
        within = at & 7
        picked = jnp.zeros((8, lanes), F32)
        for start in range(0, mol_count, mol_tile):
            s = nn(mol_ref[start : start + mol_tile, :], qt)
            for r in range(0, mol_tile, 8):
                taken = jnp.take_along_axis(s[r : r + 8], within, axis=0)
                picked = jnp.where(group == (start + r) // 8, taken, picked)
        cs = picked[0:4]
        d = nn(bank_ref[...], qt)
        bs_ref[:, cols] = d
        masked = jnp.where(here_at >= 0, cs, -1e30)
        best = jnp.maximum(
            jnp.max(d, axis=0, keepdims=True), jnp.max(masked, axis=0, keepdims=True)
        )
        total = jnp.sum(jnp.exp2((masked - best) * INV_LOG2), axis=0, keepdims=True)
        e = jnp.exp2((bs_ref[:, cols] - best) * INV_LOG2)
        wbt_ref[:, out] = e.astype(BF16)
        total = total + jnp.sum(e, axis=0, keepdims=True)
        zero = jnp.zeros((1, lanes), F32)
        sent = jnp.concatenate(
            [best * INV + jnp.log(total), jnp.where(here_at[0:1] >= 0, cs[0:1] * INV, 0.0)], axis=0
        )
        lse_ref[:, out] = sent
        st_ref[:, out] = jnp.concatenate(
            [best * INV, zero, zero, zero, cs * INV, here_at, norm, zero, zero, zero], axis=0
        )


def bank_kernel(whole, pair, bankt_ref, wbt_ref, acc_ref):
    cols = pl.ds(pl.multiple_of(pl.program_id(0) * pair, 256), pair) if whole else slice(None)
    acc_ref[:, cols] = nn(bankt_ref[...], wbt_ref[:, cols])


def grad_kernel(rows, lanes, whole, lib_size, mine_ref, *refs):
    lse_refs = refs[:lib_size]
    st_ref, qt_ref, sp_ref, acc_ref, molt_ref = refs[lib_size : lib_size + 5]
    refs = refs[lib_size + 5 :]
    gt_ref, loss_ref = refs[:2]
    gw_refs = refs[2 : 2 + lib_size]
    dq_ref, gwt_ref, block_ref = refs[-3:]
    p = pl.program_id(0)
    last = pl.num_programs(0) - 1
    pair = 2 * rows
    mol_count = molt_ref.shape[1]
    start = pl.multiple_of(p * pair, 256) if whole else 0
    here = pl.ds(start, pair)
    parts = []
    for m in range(lib_size):
        r = lse_refs[m][:, pl.ds(pl.multiple_of((p ^ (m >> 1)) * pair, 256), pair)]
        if m & 1:
            r = jnp.concatenate([r[:, rows:], r[:, :rows]], axis=1)
        parts.append(r)
    top = parts[0][0:1]
    for r in parts[1:]:
        top = jnp.maximum(top, r[0:1])
    total = tree([jnp.exp(r[0:1] - top) for r in parts])
    cs0 = tree([r[1:2] for r in parts])
    lse = top + jnp.log(total)
    terms = lse - cs0
    for half in range(2):
        block_ref[pl.ds(2 * p + half, 1), :] = jnp.broadcast_to(
            jnp.sum(terms[:, half * rows : (half + 1) * rows]), (1, block_ref.shape[1])
        )

    st = st_ref[:, here]
    inv_norm = 1.0 / st[12:13]
    at = [st[8 + j : 9 + j].astype(jnp.int32) for j in range(4)]
    g = []
    for j in range(4):
        e = jnp.exp(st[4 + j : 5 + j] - lse)
        g.append(jnp.where(at[j] >= 0, e - (1.0 if j == 0 else 0.0), 0.0))
    for j in range(1, 4):
        for k in range(j):
            same = (at[j] == at[k]) & (at[j] >= 0)
            g[k] = g[k] + jnp.where(same, g[j], 0.0)
            at[j] = jnp.where(same, -1, at[j])
    row = lax.broadcasted_iota(jnp.int16, (16, lanes), 0)
    for c in range(0, pair, lanes):
        cols = slice(c, c + lanes)
        out = pl.ds(start + c, lanes)
        gap = [
            jnp.broadcast_to(at[j][:, cols], (16, lanes)).astype(jnp.int16) - row for j in range(4)
        ]
        put = [jnp.broadcast_to(g[j][:, cols], (16, lanes)).astype(BF16) for j in range(4)]
        for r in range(0, mol_count, 16):
            w = jnp.zeros((16, lanes), BF16)
            for j in range(4):
                w = jnp.where(gap[j] == jnp.int16(r), put[j], w)
            gt_ref[r : r + 16, out] = w
        dq_ref[:, cols] = nn(molt_ref[...], gt_ref[:, out])
    scale = jnp.exp(st[0:1] - lse)
    dq = dq_ref[...] + acc_ref[:, here] * scale
    unit = qt_ref[:, here].astype(F32)
    along = jnp.sum(unit * dq, axis=0, keepdims=True)
    du = ((dq - unit * along) * (inv_norm * INV)).astype(BF16)
    part = nn(du, sp_ref[here, :])

    @pl.when(p == 0)
    def _():
        gwt_ref[...] = jnp.zeros_like(gwt_ref)

    gwt_ref[...] += part

    if not whole:
        gm_ref = refs[2 + lib_size]

        @pl.when(p == 0)
        def _():
            gm_ref[...] = jnp.zeros_like(gm_ref)

        gm_ref[...] += nt(gt_ref[...], qt_ref[...]) * INV

    @pl.when(p == last)
    def _():
        gwt_ref[...] = gwt_ref[...].T
        for m in range(lib_size):
            chunk = gw_refs[m].shape[0]
            start = pl.multiple_of((mine_ref[0] ^ m) * chunk, chunk)
            gw_refs[m][...] = gwt_ref[pl.ds(start, chunk), :].astype(BF16)
        left = jnp.broadcast_to(
            tree([block_ref[m : m + 1, :] for m in range(lib_size)]), (16, block_ref.shape[1])
        )
        split = []
        for _ in range(3):
            part_of = left.astype(BF16).astype(F32)
            split.append(part_of)
            left = left - part_of
        spot = lax.broadcasted_iota(jnp.int32, left.shape, 0)
        row = jnp.where(spot == 0, split[0], jnp.where(spot == 1, split[1], split[2]))
        loss_ref[...] = jnp.where(spot < 3, row, 0.0).astype(BF16)


def mol_kernel(first, gt_ref, qt_ref, *refs):
    out_ref = refs[-1]
    out_ref[...] = nt(gt_ref[first : first + out_ref.shape[0], :], qt_ref[...]) * INV


def fold_kernel(loss_ref, *refs):
    out_ref = refs[-1]
    chunk = refs[0].shape[0]
    out_ref[:chunk, :] = tree([r[...].astype(F32) for r in refs[:-1]]).astype(BF16)
    out_ref[chunk:, :] = loss_ref[...]


def share_kernel(*refs):
    out_ref, loss_ref = refs[-2:]
    chunk = out_ref.shape[0]
    total = tree([r[...].astype(F32) for r in refs[:-2]])
    out_ref[...] = total[:chunk].astype(BF16)
    loss = total[chunk : chunk + 1] + total[chunk + 1 : chunk + 2] + total[chunk + 2 : chunk + 3]
    loss_ref[...] = jnp.broadcast_to(loss[:, :128], loss_ref.shape)


def place_kernel(mine_ref, *refs):
    out_ref = refs[-1]
    for m, r in enumerate(refs[:-1]):
        start = pl.multiple_of((mine_ref[0] ^ m) * r.shape[0], r.shape[0])
        out_ref[pl.ds(start, r.shape[0]), :] = r[...].astype(F32)


def params(limit=VMEM_BYTES, **kw):
    return pltpu.CompilerParams(vmem_limit_bytes=limit, **kw)


def cost(flops, nbytes):
    return pl.CostEstimate(flops=flops, bytes_accessed=nbytes, transcendentals=0)


def per_device(spectra, w_proj, fixed_library_matrix, mol_rows, cand_ids, iso_count):
    rows, width = spectra.shape
    mol_count = mol_rows.shape[0]
    bank_count = fixed_library_matrix.shape[0]
    lib_size = lax.axis_size("lib")
    dp_size = lax.axis_size("dp")
    columns = cand_ids.shape[1]
    pairs = lib_size // 2
    pair = 2 * rows
    n = pairs * pair
    me = lax.axis_index("lib").astype(jnp.int32)[None]
    full = pl.BlockSpec(memory_space=pltpu.VMEM)
    smem = pl.BlockSpec(memory_space=pltpu.SMEM)
    anywhere = pl.BlockSpec(memory_space=pl.ANY)
    sds = jax.ShapeDtypeStruct
    held = n * (2 * width + 2 * width + 2 * mol_count + 2 * bank_count + 4 * width)
    whole = held <= ROOM_BYTES

    column = jnp.arange(columns, dtype=jnp.int32)[:, None]
    ids = cand_ids.T % (lib_size * mol_count)
    dead = column > iso_count[None, :]
    high = jnp.where(dead, -1, ids // BASE)
    low = ids % BASE
    digits = jnp.concatenate([high, low], axis=0).astype(BF16)
    digits = jnp.pad(digits, ((0, 16 - 2 * columns), (0, width - rows)))
    own = jnp.concatenate([spectra, digits], axis=0)
    own, me = lax.optimization_barrier((own, me))

    def swap(x, mask):
        return lax.ppermute(x, "lib", [(i, i ^ mask) for i in range(lib_size)])

    blocks = [own] + [None] * (lib_size - 1)
    for k in range(2, lib_size, 2):
        blocks[k] = swap(own, k)
    blocks[1] = swap(own, 1)
    for k in range(2, lib_size, 2):
        blocks[k + 1] = swap(blocks[k], 1)

    outs = [
        ((width, n), BF16, (width, pair), lambda p: (0, p)),
        ((n, width), BF16, (pair, width), lambda p: (p, 0)),
        ((bank_count, n), BF16, (bank_count, pair), lambda p: (0, p)),
        ((16, n), F32, (16, pair), lambda p: (0, p)),
        ((2, n), F32, (2, pair), lambda p: (0, p)),
    ]
    spec_q, spec_s, spec_w, spec_st = [full if whole else pl.BlockSpec(b, f) for _, _, b, f in outs[:4]]
    spec_acc = spec_q
    state = []
    for p in range(pairs):
        state = pl.pallas_call(
            functools.partial(score_kernel, rows, 256, 1024, p * pair if whole else 0, len(state)),
            grid=(1,),
            in_specs=[smem] + [full] * 5 + [anywhere] * len(state),
            out_specs=[
                full if whole else pl.BlockSpec(b, functools.partial(lambda f, p, i: f(p), f, p))
                for _, _, b, f in outs
            ],
            out_shape=[sds(s, d) for s, d, _, _ in outs],
            scratch_shapes=[pltpu.VMEM((bank_count, pair), F32), pltpu.VMEM((width, width), BF16)],
            input_output_aliases={6 + i: i for i in range(len(state))},
            compiler_params=params(),
            cost_estimate=cost(2 * pair * width * (width + bank_count + mol_count), 8 << 20),
            name="score",
        )(me, blocks[2 * p], blocks[2 * p + 1], w_proj, fixed_library_matrix, mol_rows, *state)
    q_t, spec_all, wb_t, st, lse_own = state

    lse_all = [lse_own] + [swap(lse_own, m) for m in range(1, lib_size)]

    bank_t, mol_t = pl.pallas_call(
        turn_kernel,
        in_specs=[full] * 2,
        out_specs=[full] * 2,
        out_shape=[sds((a.shape[1], a.shape[0]), BF16) for a in (fixed_library_matrix, mol_rows)],
        compiler_params=params(),
        cost_estimate=cost(0, 8 << 20),
        name="turn",
    )(fixed_library_matrix, mol_rows)

    acc = pl.pallas_call(
        functools.partial(bank_kernel, whole, pair),
        grid=(pairs,),
        in_specs=[full, spec_w],
        out_specs=spec_acc,
        out_shape=sds((width, n), F32),
        compiler_params=params(),
        cost_estimate=cost(2 * n * width * bank_count, 14 << 20),
        name="bank",
    )(bank_t, wb_t)

    chunk = width // lib_size
    grad_outs = [sds((mol_count, n if whole else pair), BF16), sds((16, width), BF16)]
    grad_outs += [sds((chunk, width), BF16)] * lib_size
    if not whole:
        grad_outs.append(sds((mol_count, width), F32))
    grads = pl.pallas_call(
        functools.partial(grad_kernel, rows, 256, whole, lib_size),
        grid=(pairs,),
        in_specs=[smem] + [full] * lib_size + [spec_st, spec_q, spec_s, spec_acc, full],
        out_specs=[full] * len(grad_outs),
        out_shape=grad_outs,
        scratch_shapes=[
            pltpu.VMEM((width, pair), F32),
            pltpu.VMEM((width, width), F32),
            pltpu.VMEM((lib_size, width), F32),
        ],
        compiler_params=params() if whole else params(40 << 20),
        cost_estimate=cost(2 * n * width * (mol_count + width), 24 << 20),
        name="grad",
    )(me, *lse_all, st, q_t, spec_all, acc, mol_t)
    g_t, loss_part = grads[:2]
    gw_parts = grads[2 : 2 + lib_size]

    if whole:
        piece = mol_count // PIECES
        grad_mol = []
        for r in range(PIECES):
            grad_mol = [
                pl.pallas_call(
                    functools.partial(mol_kernel, r * piece),
                    grid=(1,),
                    in_specs=[full, full] + [anywhere] * len(grad_mol),
                    out_specs=pl.BlockSpec((piece, width), functools.partial(lambda r, i: (r, 0), r)),
                    out_shape=pltpu.HBM((mol_count, width), F32),
                    input_output_aliases={2: 0} if grad_mol else {},
                    compiler_params=params(),
                    cost_estimate=cost(2 * n * width * piece, 7 << 20),
                    name="mol",
                )(g_t, q_t, *[pltpu.with_memory_space_constraint(x, pltpu.HBM) for x in grad_mol])
            ]
        grad_mol = grad_mol[0]
    else:
        grad_mol = grads[-1]

    got = [gw_parts[0]] + [swap(gw_parts[m], m) for m in range(1, lib_size)]
    sent = pl.pallas_call(
        fold_kernel,
        in_specs=[full] * (1 + lib_size),
        out_specs=full,
        out_shape=sds((chunk + 16, width), BF16),
        compiler_params=params(8 << 20),
        cost_estimate=cost(0, 1 << 20),
        name="fold",
    )(loss_part, *got)
    terms = [sent]
    for k in range(1, dp_size):
        terms.append(lax.ppermute(sent, "dp", [(i, i ^ k) for i in range(dp_size)]))
    shared, loss_sum = pl.pallas_call(
        share_kernel,
        in_specs=[full] * dp_size,
        out_specs=[full, full],
        out_shape=[sds((chunk, width), BF16), sds((8, 128), F32)],
        compiler_params=params(8 << 20),
        cost_estimate=cost(0, 1 << 20),
        name="share",
    )(*terms)
    everyone = [shared] + [swap(shared, m) for m in range(1, lib_size)]
    grad_w = pl.pallas_call(
        place_kernel,
        in_specs=[smem] + [full] * lib_size,
        out_specs=full,
        out_shape=pltpu.HBM((width, width), F32),
        compiler_params=params(8 << 20),
        cost_estimate=cost(0, 2 << 20),
        name="place",
    )(me, *everyone)
    loss = loss_sum[0, 0] / (rows * dp_size * lib_size)
    return (grad_w, grad_mol, loss)


def solution(mesh):
    placed = (
        P(("dp", "lib"), None),
        P(),
        P("lib", None),
        P(("dp", "lib"), None),
        P(("dp", "lib"), None),
        P(("dp", "lib")),
    )

    return jax.shard_map(
        per_device,
        mesh=mesh,
        in_specs=placed,
        out_specs=(P(), P(("dp", "lib"), None), P()),
        check_vma=False,
    )
```

```python
import functools

import jax
import jax.numpy as jnp
from jax import lax
from jax.experimental import pallas as pl
from jax.experimental.pallas import tpu as pltpu
from jax.sharding import PartitionSpec as P


sharpness_divisor = 0.07
INV = 1.0 / sharpness_divisor
INV_LOG2 = 1.4426950408889634 / sharpness_divisor
BASE = 256
F32 = jnp.float32
BF16 = jnp.bfloat16
VMEM_BYTES = 16 * 1024 * 1024
ROOM_BYTES = 36 * 1024 * 1024
PIECES = ((0, 2), (4, 4), (2, 2))


def nt(a, b):
    return lax.dot_general(a, b, (((1,), (1,)), ((), ())), preferred_element_type=F32)


def nn(a, b):
    return lax.dot_general(a, b, (((1,), (0,)), ((), ())), preferred_element_type=F32)


def tree(terms):
    while len(terms) > 1:
        terms = [a + b for a, b in zip(terms[::2], terms[1::2])]
    return terms[0]


def turn_kernel(bank_ref, mol_ref, bankt_ref, molt_ref):
    for src, dst in ((bank_ref, bankt_ref), (mol_ref, molt_ref)):
        for r in range(0, src.shape[0], 256):
            dst[:, r : r + 256] = src[r : r + 256, :].T


def load_kernel(digits_ref, spec_ref, *refs):
    count = (len(refs) - 2) // 2
    sems = refs[-1]
    own_ref = refs[count]
    moves = [pltpu.make_async_copy(spec_ref, own_ref.at[: spec_ref.shape[0]], sems.at[count])]
    for i in range(count):
        moves.append(pltpu.make_async_copy(refs[i], refs[count + 1 + i], sems.at[i]))
    for move in moves:
        move.start()
    own_ref[spec_ref.shape[0] :, :] = digits_ref[...]
    for move in moves:
        move.wait()


def score_kernel(rows, lanes, mol_tile, at_lane, aliased, *refs):
    own_ref, xa_ref, xb_ref, w_ref, bank_ref, mol_ref = refs[:6]
    refs = refs[6 + aliased :]
    qt_ref, sp_ref, wbt_ref, st_ref, lse_ref, bs_ref, wt_ref = refs
    mol_count = mol_ref.shape[0]
    pair = 2 * rows
    sp_ref[at_lane : at_lane + rows, :] = xa_ref[:rows, :]
    sp_ref[at_lane + rows : at_lane + pair, :] = xb_ref[:rows, :]
    wt_ref[...] = w_ref[...].T
    digits = jnp.concatenate(
        [xa_ref[rows : rows + 16, :rows].astype(F32), xb_ref[rows : rows + 16, :rows].astype(F32)],
        axis=1,
    )
    base = (own_ref[0] * mol_count).astype(F32)
    local = digits[0:4] * BASE + digits[4:8] - base
    local = jnp.where((local >= 0) & (local < mol_count), local, -1.0)
    for c in range(0, pair, lanes):
        cols = slice(c, c + lanes)
        out = slice(at_lane + c, at_lane + c + lanes)
        ut = nt(wt_ref[...], sp_ref[out, :])
        norm = jnp.sqrt(jnp.sum(ut * ut, axis=0, keepdims=True) + 1e-06)
        qt = (ut * (1.0 / norm)).astype(BF16)
        qt_ref[:, out] = qt
        here_at = local[:, cols]
        at = here_at.astype(jnp.int32)
        at = jnp.concatenate([at, at], axis=0)
        group = at >> 3
        within = at & 7
        picked = jnp.zeros((8, lanes), F32)
        for start in range(0, mol_count, mol_tile):
            s = nn(mol_ref[start : start + mol_tile, :], qt)
            for r in range(0, mol_tile, 8):
                taken = jnp.take_along_axis(s[r : r + 8], within, axis=0)
                picked = jnp.where(group == (start + r) // 8, taken, picked)
        cs = picked[0:4]
        d = nn(bank_ref[...], qt)
        bs_ref[:, cols] = d
        masked = jnp.where(here_at >= 0, cs, -1e30)
        best = jnp.maximum(
            jnp.max(d, axis=0, keepdims=True), jnp.max(masked, axis=0, keepdims=True)
        )
        total = jnp.sum(jnp.exp2((masked - best) * INV_LOG2), axis=0, keepdims=True)
        e = jnp.exp2((bs_ref[:, cols] - best) * INV_LOG2)
        wbt_ref[:, out] = e.astype(BF16)
        total = total + jnp.sum(e, axis=0, keepdims=True)
        zero = jnp.zeros((1, lanes), F32)
        sent = jnp.concatenate(
            [best * INV + jnp.log(total), jnp.where(here_at[0:1] >= 0, cs[0:1] * INV, 0.0)], axis=0
        )
        lse_ref[:, out] = sent
        st_ref[:, out] = jnp.concatenate(
            [best * INV, zero, zero, zero, cs * INV, here_at, norm, zero, zero, zero], axis=0
        )


def bank_kernel(whole, pair, bankt_ref, wbt_ref, acc_ref):
    cols = pl.ds(pl.multiple_of(pl.program_id(0) * pair, 256), pair) if whole else slice(None)
    acc_ref[:, cols] = nn(bankt_ref[...], wbt_ref[:, cols])


def grad_kernel(rows, lanes, whole, lib_size, mine_ref, *refs):
    lse_refs = refs[:lib_size]
    st_ref, qt_ref, sp_ref, acc_ref, molt_ref = refs[lib_size : lib_size + 5]
    refs = refs[lib_size + 5 :]
    gt_ref, loss_ref = refs[:2]
    gw_refs = refs[2 : 2 + lib_size]
    dq_ref, gwt_ref, block_ref = refs[-3:]
    p = pl.program_id(0)
    last = pl.num_programs(0) - 1
    pair = 2 * rows
    mol_count = molt_ref.shape[1]
    start = pl.multiple_of(p * pair, 256) if whole else 0
    here = pl.ds(start, pair)
    parts = []
    for m in range(lib_size):
        r = lse_refs[m][:, pl.ds(pl.multiple_of((p ^ (m >> 1)) * pair, 256), pair)]
        if m & 1:
            r = jnp.concatenate([r[:, rows:], r[:, :rows]], axis=1)
        parts.append(r)
    top = parts[0][0:1]
    for r in parts[1:]:
        top = jnp.maximum(top, r[0:1])
    total = tree([jnp.exp(r[0:1] - top) for r in parts])
    cs0 = tree([r[1:2] for r in parts])
    lse = top + jnp.log(total)
    terms = lse - cs0
    for half in range(2):
        block_ref[pl.ds(2 * p + half, 1), :] = jnp.broadcast_to(
            jnp.sum(terms[:, half * rows : (half + 1) * rows]), (1, block_ref.shape[1])
        )

    st = st_ref[:, here]
    inv_norm = 1.0 / st[12:13]
    at = [st[8 + j : 9 + j].astype(jnp.int32) for j in range(4)]
    g = []
    for j in range(4):
        e = jnp.exp(st[4 + j : 5 + j] - lse)
        g.append(jnp.where(at[j] >= 0, e - (1.0 if j == 0 else 0.0), 0.0))
    for j in range(1, 4):
        for k in range(j):
            same = (at[j] == at[k]) & (at[j] >= 0)
            g[k] = g[k] + jnp.where(same, g[j], 0.0)
            at[j] = jnp.where(same, -1, at[j])
    row = lax.broadcasted_iota(jnp.int16, (16, lanes), 0)
    for c in range(0, pair, lanes):
        cols = slice(c, c + lanes)
        out = pl.ds(start + c, lanes)
        gap = [
            jnp.broadcast_to(at[j][:, cols], (16, lanes)).astype(jnp.int16) - row for j in range(4)
        ]
        put = [jnp.broadcast_to(g[j][:, cols], (16, lanes)).astype(BF16) for j in range(4)]
        for r in range(0, mol_count, 16):
            w = jnp.zeros((16, lanes), BF16)
            for j in range(4):
                w = jnp.where(gap[j] == jnp.int16(r), put[j], w)
            gt_ref[r : r + 16, out] = w
        dq_ref[:, cols] = nn(molt_ref[...], gt_ref[:, out])
    scale = jnp.exp(st[0:1] - lse)
    dq = dq_ref[...] + acc_ref[:, here] * scale
    unit = qt_ref[:, here].astype(F32)
    along = jnp.sum(unit * dq, axis=0, keepdims=True)
    du = ((dq - unit * along) * (inv_norm * INV)).astype(BF16)
    part = nn(du, sp_ref[here, :])

    @pl.when(p == 0)
    def _():
        gwt_ref[...] = jnp.zeros_like(gwt_ref)

    gwt_ref[...] += part

    if not whole:
        gm_ref = refs[2 + lib_size]

        @pl.when(p == 0)
        def _():
            gm_ref[...] = jnp.zeros_like(gm_ref)

        gm_ref[...] += nt(gt_ref[...], qt_ref[...]) * INV

    @pl.when(p == last)
    def _():
        gwt_ref[...] = gwt_ref[...].T
        for m in range(lib_size):
            chunk = gw_refs[m].shape[0]
            start = pl.multiple_of((mine_ref[0] ^ m) * chunk, chunk)
            gw_refs[m][...] = gwt_ref[pl.ds(start, chunk), :].astype(BF16)
        left = jnp.broadcast_to(
            tree([block_ref[m : m + 1, :] for m in range(lib_size)]), (16, block_ref.shape[1])
        )
        split = []
        for _ in range(3):
            part_of = left.astype(BF16).astype(F32)
            split.append(part_of)
            left = left - part_of
        spot = lax.broadcasted_iota(jnp.int32, left.shape, 0)
        row = jnp.where(spot == 0, split[0], jnp.where(spot == 1, split[1], split[2]))
        loss_ref[...] = jnp.where(spot < 3, row, 0.0).astype(BF16)


def mol_kernel(first, gt_ref, qt_ref, *refs):
    out_ref = refs[-1]
    out_ref[...] = nt(gt_ref[first : first + out_ref.shape[0], :], qt_ref[...]) * INV


def fold_kernel(loss_ref, *refs):
    out_ref = refs[-1]
    chunk = refs[0].shape[0]
    out_ref[:chunk, :] = tree([r[...].astype(F32) for r in refs[:-1]]).astype(BF16)
    out_ref[chunk:, :] = loss_ref[...]


def share_kernel(count, *refs):
    out_ref, loss_ref = refs[-2:]
    chunk = out_ref.shape[0]
    total = tree([r[...].astype(F32) for r in refs[:-2]])
    out_ref[...] = total[:chunk].astype(BF16)
    loss = total[chunk : chunk + 1] + total[chunk + 1 : chunk + 2] + total[chunk + 2 : chunk + 3]
    loss_ref[0, 0] = jnp.max(loss) / count


def place_kernel(mine_ref, *refs):
    out_ref = refs[-1]
    for m, r in enumerate(refs[:-1]):
        start = pl.multiple_of((mine_ref[0] ^ m) * r.shape[0], r.shape[0])
        out_ref[pl.ds(start, r.shape[0]), :] = r[...].astype(F32)


def params(limit=VMEM_BYTES, **kw):
    return pltpu.CompilerParams(vmem_limit_bytes=limit, **kw)


def cost(flops, nbytes):
    return pl.CostEstimate(flops=flops, bytes_accessed=nbytes, transcendentals=0)


def per_device(spectra, w_proj, fixed_library_matrix, mol_rows, cand_ids, iso_count):
    rows, width = spectra.shape
    mol_count = mol_rows.shape[0]
    bank_count = fixed_library_matrix.shape[0]
    lib_size = lax.axis_size("lib")
    dp_size = lax.axis_size("dp")
    columns = cand_ids.shape[1]
    pairs = lib_size // 2
    pair = 2 * rows
    n = pairs * pair
    me = lax.axis_index("lib").astype(jnp.int32)[None]
    full = pl.BlockSpec(memory_space=pltpu.VMEM)
    smem = pl.BlockSpec(memory_space=pltpu.SMEM)
    anywhere = pl.BlockSpec(memory_space=pl.ANY)
    sds = jax.ShapeDtypeStruct
    held = n * (2 * width + 2 * width + 2 * mol_count + 2 * bank_count + 4 * width)
    whole = held <= ROOM_BYTES

    column = jnp.arange(columns, dtype=jnp.int32)[:, None]
    ids = cand_ids.T % (lib_size * mol_count)
    dead = column > iso_count[None, :]
    high = jnp.where(dead, -1, ids // BASE)
    low = ids % BASE
    digits = jnp.concatenate([high, low], axis=0).astype(BF16)
    digits = jnp.pad(digits, ((0, 16 - 2 * columns), (0, width - rows)))
    digits, me = lax.optimization_barrier((digits, me))
    fixed = (w_proj, fixed_library_matrix, mol_rows)
    own, *fixed = pl.pallas_call(
        load_kernel,
        in_specs=[full] + [anywhere] * 4,
        out_specs=[full] * 4,
        out_shape=[sds((rows + 16, width), BF16)] + [sds(a.shape, BF16) for a in fixed],
        scratch_shapes=[pltpu.SemaphoreType.DMA((4,))],
        compiler_params=params(),
        cost_estimate=cost(0, 4 << 20),
        name="load",
    )(digits, *[pltpu.with_memory_space_constraint(a, pltpu.HBM) for a in (spectra, *fixed)])
    w_proj, fixed_library_matrix, mol_rows = fixed

    def swap(x, mask):
        return lax.ppermute(x, "lib", [(i, i ^ mask) for i in range(lib_size)])

    blocks = [own] + [None] * (lib_size - 1)
    for k in range(2, lib_size, 2):
        blocks[k] = swap(own, k)
    blocks[1] = swap(own, 1)
    for k in range(2, lib_size, 2):
        blocks[k + 1] = swap(blocks[k], 1)

    outs = [
        ((width, n), BF16, (width, pair), lambda p: (0, p)),
        ((n, width), BF16, (pair, width), lambda p: (p, 0)),
        ((bank_count, n), BF16, (bank_count, pair), lambda p: (0, p)),
        ((16, n), F32, (16, pair), lambda p: (0, p)),
        ((2, n), F32, (2, pair), lambda p: (0, p)),
    ]
    spec_q, spec_s, spec_w, spec_st = [full if whole else pl.BlockSpec(b, f) for _, _, b, f in outs[:4]]
    spec_acc = spec_q
    state = []
    for p in range(pairs):
        state = pl.pallas_call(
            functools.partial(score_kernel, rows, 256, 1024, p * pair if whole else 0, len(state)),
            grid=(1,),
            in_specs=[smem] + [full] * 5 + [anywhere] * len(state),
            out_specs=[
                full if whole else pl.BlockSpec(b, functools.partial(lambda f, p, i: f(p), f, p))
                for _, _, b, f in outs
            ],
            out_shape=[sds(s, d) for s, d, _, _ in outs],
            scratch_shapes=[pltpu.VMEM((bank_count, pair), F32), pltpu.VMEM((width, width), BF16)],
            input_output_aliases={6 + i: i for i in range(len(state))},
            compiler_params=params(),
            cost_estimate=cost(2 * pair * width * (width + bank_count + mol_count), 8 << 20),
            name="score",
        )(me, blocks[2 * p], blocks[2 * p + 1], w_proj, fixed_library_matrix, mol_rows, *state)
    q_t, spec_all, wb_t, st, lse_own = state

    lse_all = [lse_own] + [swap(lse_own, m) for m in range(1, lib_size)]

    bank_t, mol_t = pl.pallas_call(
        turn_kernel,
        in_specs=[full] * 2,
        out_specs=[full] * 2,
        out_shape=[sds((a.shape[1], a.shape[0]), BF16) for a in (fixed_library_matrix, mol_rows)],
        compiler_params=params(),
        cost_estimate=cost(0, 8 << 20),
        name="turn",
    )(fixed_library_matrix, mol_rows)

    acc = pl.pallas_call(
        functools.partial(bank_kernel, whole, pair),
        grid=(pairs,),
        in_specs=[full, spec_w],
        out_specs=spec_acc,
        out_shape=sds((width, n), F32),
        compiler_params=params(),
        cost_estimate=cost(2 * n * width * bank_count, 14 << 20),
        name="bank",
    )(bank_t, wb_t)

    chunk = width // lib_size
    grad_outs = [sds((mol_count, n if whole else pair), BF16), sds((16, width), BF16)]
    grad_outs += [sds((chunk, width), BF16)] * lib_size
    if not whole:
        grad_outs.append(sds((mol_count, width), F32))
    grads = pl.pallas_call(
        functools.partial(grad_kernel, rows, pair, whole, lib_size),
        grid=(pairs,),
        in_specs=[smem] + [full] * lib_size + [spec_st, spec_q, spec_s, spec_acc, full],
        out_specs=[full] * len(grad_outs),
        out_shape=grad_outs,
        scratch_shapes=[
            pltpu.VMEM((width, pair), F32),
            pltpu.VMEM((width, width), F32),
            pltpu.VMEM((lib_size, width), F32),
        ],
        compiler_params=params() if whole else params(40 << 20),
        cost_estimate=cost(2 * n * width * (mol_count + width), 24 << 20),
        name="grad",
    )(me, *lse_all, st, q_t, spec_all, acc, mol_t)
    g_t, loss_part = grads[:2]
    gw_parts = grads[2 : 2 + lib_size]

    if whole:
        grad_mol = []
        for first, piece in PIECES:
            first, piece = mol_count * first // 8, mol_count * piece // 8
            grad_mol = [
                pl.pallas_call(
                    functools.partial(mol_kernel, first),
                    grid=(1,),
                    in_specs=[full, full] + [anywhere] * len(grad_mol),
                    out_specs=pl.BlockSpec(
                        (piece, width), functools.partial(lambda at, i: (at, 0), first // piece)
                    ),
                    out_shape=pltpu.HBM((mol_count, width), F32),
                    input_output_aliases={2: 0} if grad_mol else {},
                    compiler_params=params(),
                    cost_estimate=cost(2 * n * width * piece, 7 << 20),
                    name="mol",
                )(g_t, q_t, *[pltpu.with_memory_space_constraint(x, pltpu.HBM) for x in grad_mol])
            ]
        grad_mol = grad_mol[0]
    else:
        grad_mol = grads[-1]

    got = [gw_parts[0]] + [swap(gw_parts[m], m) for m in range(1, lib_size)]
    sent = pl.pallas_call(
        fold_kernel,
        in_specs=[full] * (1 + lib_size),
        out_specs=full,
        out_shape=sds((chunk + 16, width), BF16),
        compiler_params=params(8 << 20),
        cost_estimate=cost(0, 1 << 20),
        name="fold",
    )(loss_part, *got)
    terms = [sent]
    for k in range(1, dp_size):
        terms.append(lax.ppermute(sent, "dp", [(i, i ^ k) for i in range(dp_size)]))
    shared, loss_sum = pl.pallas_call(
        functools.partial(share_kernel, rows * dp_size * lib_size),
        in_specs=[full] * dp_size,
        out_specs=[full, smem],
        out_shape=[sds((chunk, width), BF16), sds((1, 1), F32)],
        compiler_params=params(8 << 20),
        cost_estimate=cost(0, 1 << 20),
        name="share",
    )(*terms)
    everyone = [shared] + [swap(shared, m) for m in range(1, lib_size)]
    grad_w = pl.pallas_call(
        place_kernel,
        in_specs=[smem] + [full] * lib_size,
        out_specs=full,
        out_shape=pltpu.HBM((width, width), F32),
        compiler_params=params(8 << 20),
        cost_estimate=cost(0, 2 << 20),
        name="place",
    )(me, *everyone)
    loss = loss_sum.reshape(())
    return (grad_w, grad_mol, loss)


def solution(mesh):
    placed = (
        P(("dp", "lib"), None),
        P(),
        P("lib", None),
        P(("dp", "lib"), None),
        P(("dp", "lib"), None),
        P(("dp", "lib")),
    )

    return jax.shard_map(
        per_device,
        mesh=mesh,
        in_specs=placed,
        out_specs=(P(), P(("dp", "lib"), None), P()),
        check_vma=False,
    )
```

```python
import functools

import jax
import jax.numpy as jnp
from jax import lax
from jax.experimental import pallas as pl
from jax.experimental.pallas import tpu as pltpu
from jax.sharding import PartitionSpec as P


sharpness_divisor = 0.07
INV = 1.0 / sharpness_divisor
INV_LOG2 = 1.4426950408889634 / sharpness_divisor
BASE = 256
F32 = jnp.float32
BF16 = jnp.bfloat16
VMEM_BYTES = 16 * 1024 * 1024
ROOM_BYTES = 36 * 1024 * 1024
PIECES = ((0, 2), (4, 4), (2, 2))


def nt(a, b):
    return lax.dot_general(a, b, (((1,), (1,)), ((), ())), preferred_element_type=F32)


def nn(a, b):
    return lax.dot_general(a, b, (((1,), (0,)), ((), ())), preferred_element_type=F32)


def tree(terms):
    while len(terms) > 1:
        terms = [a + b for a, b in zip(terms[::2], terms[1::2])]
    return terms[0]


def turn_kernel(bank_ref, mol_ref, bankt_ref, molt_ref):
    for src, dst in ((bank_ref, bankt_ref), (mol_ref, molt_ref)):
        for r in range(0, src.shape[0], 256):
            dst[:, r : r + 256] = src[r : r + 256, :].T


def load_kernel(digits_ref, spec_ref, *refs):
    count = (len(refs) - 2) // 2
    sems = refs[-1]
    own_ref = refs[count]
    moves = [pltpu.make_async_copy(spec_ref, own_ref.at[: spec_ref.shape[0]], sems.at[count])]
    for i in range(count):
        moves.append(pltpu.make_async_copy(refs[i], refs[count + 1 + i], sems.at[i]))
    for move in moves:
        move.start()
    own_ref[spec_ref.shape[0] :, :] = digits_ref[...]
    for move in moves:
        move.wait()


def score_kernel(rows, lanes, mol_tile, at_lane, aliased, *refs):
    own_ref, w_ref, bank_ref, mol_ref, xa_ref, xb_ref = refs[:6]
    refs = refs[6 + aliased :]
    qt_ref, sp_ref, wbt_ref, st_ref, lse_ref, bs_ref, wt_ref = refs
    mol_count = mol_ref.shape[0]
    pair = 2 * rows
    sp_ref[at_lane : at_lane + rows, :] = xa_ref[:rows, :]
    sp_ref[at_lane + rows : at_lane + pair, :] = xb_ref[:rows, :]
    wt_ref[...] = w_ref[...].T
    digits = jnp.concatenate(
        [x[rows : rows + 16, :rows].astype(F32) for x in (xa_ref, xb_ref)], axis=1
    )
    base = (own_ref[0] * mol_count).astype(F32)
    local = digits[0:4] * BASE + digits[4:8] - base
    local = jnp.where((local >= 0) & (local < mol_count), local, -1.0)
    for c in range(0, pair, lanes):
        cols = slice(c, c + lanes)
        out = slice(at_lane + c, at_lane + c + lanes)
        ut = nt(wt_ref[...], sp_ref[out, :])
        norm = jnp.sqrt(jnp.sum(ut * ut, axis=0, keepdims=True) + 1e-06)
        qt = (ut * (1.0 / norm)).astype(BF16)
        qt_ref[:, out] = qt
        here_at = local[:, cols]
        at = here_at.astype(jnp.int32)
        at = jnp.concatenate([at, at], axis=0)
        group = at >> 3
        within = at & 7
        picked = jnp.zeros((8, lanes), F32)
        for start in range(0, mol_count, mol_tile):
            s = nn(mol_ref[start : start + mol_tile, :], qt)
            for r in range(0, mol_tile, 8):
                taken = jnp.take_along_axis(s[r : r + 8], within, axis=0)
                picked = jnp.where(group == (start + r) // 8, taken, picked)
        cs = picked[0:4]
        d = nn(bank_ref[...], qt)
        bs_ref[:, cols] = d
        masked = jnp.where(here_at >= 0, cs, -1e30)
        best = jnp.maximum(
            jnp.max(d, axis=0, keepdims=True), jnp.max(masked, axis=0, keepdims=True)
        )
        total = jnp.sum(jnp.exp2((masked - best) * INV_LOG2), axis=0, keepdims=True)
        e = jnp.exp2((bs_ref[:, cols] - best) * INV_LOG2)
        wbt_ref[:, out] = e.astype(BF16)
        total = total + jnp.sum(e, axis=0, keepdims=True)
        zero = jnp.zeros((1, lanes), F32)
        sent = jnp.concatenate(
            [best * INV + jnp.log(total), jnp.where(here_at[0:1] >= 0, cs[0:1] * INV, 0.0)], axis=0
        )
        lse_ref[:, out] = sent
        st_ref[:, out] = jnp.concatenate(
            [best * INV, zero, zero, zero, cs * INV, here_at, norm, zero, zero, zero], axis=0
        )


def bank_kernel(whole, pair, first, bankt_ref, wbt_ref, *refs):
    acc_ref = refs[-1]
    at = (first + pl.program_id(0)) * pair
    cols = pl.ds(pl.multiple_of(at, 256), pair) if whole else slice(None)
    acc_ref[:, cols] = nn(bankt_ref[...], wbt_ref[:, cols])


def grad_kernel(rows, lanes, whole, lib_size, mine_ref, *refs):
    lse_refs = refs[:lib_size]
    st_ref, qt_ref, sp_ref, acc_ref, molt_ref = refs[lib_size : lib_size + 5]
    refs = refs[lib_size + 5 :]
    gt_ref, loss_ref = refs[:2]
    gw_refs = refs[2 : 2 + lib_size]
    dq_ref, gwt_ref, block_ref = refs[-3:]
    p = pl.program_id(0)
    last = pl.num_programs(0) - 1
    pair = 2 * rows
    mol_count = molt_ref.shape[1]
    start = pl.multiple_of(p * pair, 256) if whole else 0
    here = pl.ds(start, pair)
    parts = []
    for m in range(lib_size):
        r = lse_refs[m][:, pl.ds(pl.multiple_of((p ^ (m >> 1)) * pair, 256), pair)]
        if m & 1:
            r = jnp.concatenate([r[:, rows:], r[:, :rows]], axis=1)
        parts.append(r)
    top = parts[0][0:1]
    for r in parts[1:]:
        top = jnp.maximum(top, r[0:1])
    total = tree([jnp.exp(r[0:1] - top) for r in parts])
    cs0 = tree([r[1:2] for r in parts])
    lse = top + jnp.log(total)
    terms = lse - cs0
    for half in range(2):
        block_ref[pl.ds(2 * p + half, 1), :] = jnp.broadcast_to(
            jnp.sum(terms[:, half * rows : (half + 1) * rows]), (1, block_ref.shape[1])
        )

    st = st_ref[:, here]
    inv_norm = 1.0 / st[12:13]
    at = [st[8 + j : 9 + j].astype(jnp.int32) for j in range(4)]
    g = []
    for j in range(4):
        e = jnp.exp(st[4 + j : 5 + j] - lse)
        g.append(jnp.where(at[j] >= 0, e - (1.0 if j == 0 else 0.0), 0.0))
    for j in range(1, 4):
        for k in range(j):
            same = (at[j] == at[k]) & (at[j] >= 0)
            g[k] = g[k] + jnp.where(same, g[j], 0.0)
            at[j] = jnp.where(same, -1, at[j])
    row = lax.broadcasted_iota(jnp.int16, (16, lanes), 0)
    for c in range(0, pair, lanes):
        cols = slice(c, c + lanes)
        out = pl.ds(start + c, lanes)
        gap = [
            jnp.broadcast_to(at[j][:, cols], (16, lanes)).astype(jnp.int16) - row for j in range(4)
        ]
        put = [jnp.broadcast_to(g[j][:, cols], (16, lanes)).astype(BF16) for j in range(4)]
        for r in range(0, mol_count, 16):
            w = jnp.zeros((16, lanes), BF16)
            for j in range(4):
                w = jnp.where(gap[j] == jnp.int16(r), put[j], w)
            gt_ref[r : r + 16, out] = w
        dq_ref[:, cols] = nn(molt_ref[...], gt_ref[:, out])
    scale = jnp.exp(st[0:1] - lse)
    dq = dq_ref[...] + acc_ref[:, here] * scale
    unit = qt_ref[:, here].astype(F32)
    along = jnp.sum(unit * dq, axis=0, keepdims=True)
    du = ((dq - unit * along) * (inv_norm * INV)).astype(BF16)
    part = nn(du, sp_ref[here, :])

    @pl.when(p == 0)
    def _():
        gwt_ref[...] = jnp.zeros_like(gwt_ref)

    gwt_ref[...] += part

    if not whole:
        gm_ref = refs[2 + lib_size]

        @pl.when(p == 0)
        def _():
            gm_ref[...] = jnp.zeros_like(gm_ref)

        gm_ref[...] += nt(gt_ref[...], qt_ref[...]) * INV

    @pl.when(p == last)
    def _():
        gwt_ref[...] = gwt_ref[...].T
        for m in range(lib_size):
            chunk = gw_refs[m].shape[0]
            start = pl.multiple_of((mine_ref[0] ^ m) * chunk, chunk)
            gw_refs[m][...] = gwt_ref[pl.ds(start, chunk), :].astype(BF16)
        left = jnp.broadcast_to(
            tree([block_ref[m : m + 1, :] for m in range(lib_size)]), (16, block_ref.shape[1])
        )
        split = []
        for _ in range(3):
            part_of = left.astype(BF16).astype(F32)
            split.append(part_of)
            left = left - part_of
        spot = lax.broadcasted_iota(jnp.int32, left.shape, 0)
        row = jnp.where(spot == 0, split[0], jnp.where(spot == 1, split[1], split[2]))
        loss_ref[...] = jnp.where(spot < 3, row, 0.0).astype(BF16)


def mol_kernel(first, gt_ref, qt_ref, *refs):
    out_ref = refs[-1]
    out_ref[...] = nt(gt_ref[first : first + out_ref.shape[0], :], qt_ref[...]) * INV


def fold_kernel(loss_ref, *refs):
    out_ref = refs[-1]
    chunk = refs[0].shape[0]
    out_ref[:chunk, :] = tree([r[...].astype(F32) for r in refs[:-1]]).astype(BF16)
    out_ref[chunk:, :] = loss_ref[...]


def share_kernel(count, *refs):
    out_ref, loss_ref = refs[-2:]
    chunk = out_ref.shape[0]
    total = tree([r[...].astype(F32) for r in refs[:-2]])
    out_ref[...] = total[:chunk].astype(BF16)
    loss = total[chunk : chunk + 1] + total[chunk + 1 : chunk + 2] + total[chunk + 2 : chunk + 3]
    loss_ref[0, 0] = jnp.max(loss) / count


def place_kernel(mine_ref, *refs):
    out_ref = refs[-1]
    for m, r in enumerate(refs[:-1]):
        start = pl.multiple_of((mine_ref[0] ^ m) * r.shape[0], r.shape[0])
        out_ref[pl.ds(start, r.shape[0]), :] = r[...].astype(F32)


def params(limit=VMEM_BYTES, **kw):
    return pltpu.CompilerParams(vmem_limit_bytes=limit, **kw)


def cost(flops, nbytes):
    return pl.CostEstimate(flops=flops, bytes_accessed=nbytes, transcendentals=0)


def per_device(spectra, w_proj, fixed_library_matrix, mol_rows, cand_ids, iso_count):
    rows, width = spectra.shape
    mol_count = mol_rows.shape[0]
    bank_count = fixed_library_matrix.shape[0]
    lib_size = lax.axis_size("lib")
    dp_size = lax.axis_size("dp")
    columns = cand_ids.shape[1]
    pairs = lib_size // 2
    pair = 2 * rows
    n = pairs * pair
    me = lax.axis_index("lib").astype(jnp.int32)[None]
    full = pl.BlockSpec(memory_space=pltpu.VMEM)
    smem = pl.BlockSpec(memory_space=pltpu.SMEM)
    anywhere = pl.BlockSpec(memory_space=pl.ANY)
    sds = jax.ShapeDtypeStruct
    held = n * (2 * width + 2 * width + 2 * mol_count + 2 * bank_count + 4 * width)
    whole = held <= ROOM_BYTES

    column = jnp.arange(columns, dtype=jnp.int32)[:, None]
    ids = cand_ids.T % (lib_size * mol_count)
    dead = column > iso_count[None, :]
    high = jnp.where(dead, -1, ids // BASE)
    low = ids % BASE
    digits = jnp.concatenate([high, low], axis=0).astype(BF16)
    digits = jnp.pad(digits, ((0, 16 - 2 * columns), (0, width - rows)))
    digits, me = lax.optimization_barrier((digits, me))
    fixed = (w_proj, fixed_library_matrix, mol_rows)
    own, *fixed = pl.pallas_call(
        load_kernel,
        in_specs=[full] + [anywhere] * 4,
        out_specs=[full] * 4,
        out_shape=[sds((rows + 16, width), BF16)] + [sds(a.shape, BF16) for a in fixed],
        scratch_shapes=[pltpu.SemaphoreType.DMA((4,))],
        compiler_params=params(),
        cost_estimate=cost(0, 4 << 20),
        name="load",
    )(digits, *[pltpu.with_memory_space_constraint(a, pltpu.HBM) for a in (spectra, *fixed)])
    w_proj, fixed_library_matrix, mol_rows = fixed

    def swap(x, mask):
        return lax.ppermute(x, "lib", [(i, i ^ mask) for i in range(lib_size)])

    blocks = [own] + [None] * (lib_size - 1)
    for k in range(2, lib_size, 2):
        blocks[k] = swap(own, k)
    blocks[1] = swap(own, 1)
    for k in range(2, lib_size, 2):
        blocks[k + 1] = swap(blocks[k], 1)
    outs = [
        ((width, n), BF16, (width, pair), lambda p: (0, p)),
        ((n, width), BF16, (pair, width), lambda p: (p, 0)),
        ((bank_count, n), BF16, (bank_count, pair), lambda p: (0, p)),
        ((16, n), F32, (16, pair), lambda p: (0, p)),
        ((2, n), F32, (2, pair), lambda p: (0, p)),
    ]
    spec_q, spec_s, _, spec_st = [full if whole else pl.BlockSpec(b, f) for _, _, b, f in outs[:4]]
    spec_acc = spec_q

    def turn():
        return pl.pallas_call(
            turn_kernel,
            in_specs=[full] * 2,
            out_specs=[full] * 2,
            out_shape=[sds((a.shape[1], a.shape[0]), BF16) for a in (fixed_library_matrix, mol_rows)],
            compiler_params=params(),
            cost_estimate=cost(0, 8 << 20),
            name="turn",
        )(fixed_library_matrix, mol_rows)

    def bank(first, steps, wb_t, *acc):
        block_w, block_a = (
            [full, full]
            if whole
            else [pl.BlockSpec(outs[i][2], lambda p: (0, first + p)) for i in (2, 0)]
        )
        return pl.pallas_call(
            functools.partial(bank_kernel, whole, pair, first),
            grid=(steps,),
            in_specs=[full, block_w] + [anywhere] * len(acc),
            out_specs=block_a,
            out_shape=sds((width, n), F32),
            input_output_aliases={2: 0} if acc else {},
            compiler_params=params(),
            cost_estimate=cost(2 * steps * pair * width * bank_count, 14 << 20),
            name="bank",
        )(bank_t, wb_t, *acc)

    bank_t, mol_t = turn()
    state = []
    for p in range(pairs):
        state = pl.pallas_call(
            functools.partial(score_kernel, rows, 256, 1024, p * pair if whole else 0, len(state)),
            grid=(1,),
            in_specs=[smem] + [full] * 5 + [anywhere] * len(state),
            out_specs=[
                full if whole else pl.BlockSpec(b, functools.partial(lambda f, p, i: f(p), f, p))
                for _, _, b, f in outs
            ],
            out_shape=[sds(s, d) for s, d, _, _ in outs],
            scratch_shapes=[pltpu.VMEM((bank_count, pair), F32), pltpu.VMEM((width, width), BF16)],
            input_output_aliases={6 + i: i for i in range(len(state))},
            compiler_params=params(),
            cost_estimate=cost(2 * pair * width * (width + bank_count + mol_count), 8 << 20),
            name="score",
        )(me, w_proj, fixed_library_matrix, mol_rows, blocks[2 * p], blocks[2 * p + 1], *state)
        if p == 0:
            acc = bank(0, 1, state[2])
    q_t, spec_all, wb_t, st, lse_own = state

    lse_all = [lse_own] + [swap(lse_own, m) for m in range(1, lib_size)]

    acc = bank(1, pairs - 1, wb_t, acc)
    chunk = width // lib_size
    grad_outs = [sds((mol_count, n if whole else pair), BF16), sds((16, width), BF16)]
    grad_outs += [sds((chunk, width), BF16)] * lib_size
    if not whole:
        grad_outs.append(sds((mol_count, width), F32))
    grads = pl.pallas_call(
        functools.partial(grad_kernel, rows, pair, whole, lib_size),
        grid=(pairs,),
        in_specs=[smem] + [full] * lib_size + [spec_st, spec_q, spec_s, spec_acc, full],
        out_specs=[full] * len(grad_outs),
        out_shape=grad_outs,
        scratch_shapes=[
            pltpu.VMEM((width, pair), F32),
            pltpu.VMEM((width, width), F32),
            pltpu.VMEM((lib_size, width), F32),
        ],
        compiler_params=params() if whole else params(40 << 20),
        cost_estimate=cost(2 * n * width * (mol_count + width), 24 << 20),
        name="grad",
    )(me, *lse_all, st, q_t, spec_all, acc, mol_t)
    g_t, loss_part = grads[:2]
    gw_parts = grads[2 : 2 + lib_size]

    if whole:
        grad_mol = []
        for first, piece in PIECES:
            first, piece = mol_count * first // 8, mol_count * piece // 8
            grad_mol = [
                pl.pallas_call(
                    functools.partial(mol_kernel, first),
                    grid=(1,),
                    in_specs=[full, full] + [anywhere] * len(grad_mol),
                    out_specs=pl.BlockSpec(
                        (piece, width), functools.partial(lambda at, i: (at, 0), first // piece)
                    ),
                    out_shape=pltpu.HBM((mol_count, width), F32),
                    input_output_aliases={2: 0} if grad_mol else {},
                    compiler_params=params(),
                    cost_estimate=cost(2 * n * width * piece, 7 << 20),
                    name="mol",
                )(g_t, q_t, *[pltpu.with_memory_space_constraint(x, pltpu.HBM) for x in grad_mol])
            ]
        grad_mol = grad_mol[0]
    else:
        grad_mol = grads[-1]

    got = [gw_parts[0]] + [swap(gw_parts[m], m) for m in range(1, lib_size)]
    sent = pl.pallas_call(
        fold_kernel,
        in_specs=[full] * (1 + lib_size),
        out_specs=full,
        out_shape=sds((chunk + 16, width), BF16),
        compiler_params=params(8 << 20),
        cost_estimate=cost(0, 1 << 20),
        name="fold",
    )(loss_part, *got)
    terms = [sent]
    for k in range(1, dp_size):
        terms.append(lax.ppermute(sent, "dp", [(i, i ^ k) for i in range(dp_size)]))
    shared, loss_sum = pl.pallas_call(
        functools.partial(share_kernel, rows * dp_size * lib_size),
        in_specs=[full] * dp_size,
        out_specs=[full, smem],
        out_shape=[sds((chunk, width), BF16), sds((1, 1), F32)],
        compiler_params=params(8 << 20),
        cost_estimate=cost(0, 1 << 20),
        name="share",
    )(*terms)
    everyone = [shared] + [swap(shared, m) for m in range(1, lib_size)]
    grad_w = pl.pallas_call(
        place_kernel,
        in_specs=[smem] + [full] * lib_size,
        out_specs=full,
        out_shape=pltpu.HBM((width, width), F32),
        compiler_params=params(8 << 20),
        cost_estimate=cost(0, 2 << 20),
        name="place",
    )(me, *everyone)
    loss = loss_sum.reshape(())
    return (grad_w, grad_mol, loss)


def solution(mesh):
    placed = (
        P(("dp", "lib"), None),
        P(),
        P("lib", None),
        P(("dp", "lib"), None),
        P(("dp", "lib"), None),
        P(("dp", "lib")),
    )

    return jax.shard_map(
        per_device,
        mesh=mesh,
        in_specs=placed,
        out_specs=(P(), P(("dp", "lib"), None), P()),
        check_vma=False,
    )
```
